32 devices in a mesh: parts: 2 (over y), patch: 4 (over z), level: 2 (over x), sub: 2 (over core).
Axes of the slice: x: 2, y: 2, z: 4, core: 2. Of those that a mesh axis runs over, the one named last changes fastest.
Arguments:
- adjoint_height: float32 [4, 1024, 1024], P(('parts', 'level'), ('patch', 'sub')), parts along dimension 0, may hold values from -6 to 6
- adjoint_momenta: float32 [2, 4, 1024, 1024], P(None, ('parts', 'level'), ('patch', 'sub')), parts along dimension 1, may hold values from -6 to 6
- depth: float32 [2, 1024, 1024], P('level', ('patch', 'sub')), may hold values from 0.2 to 1
- wet_mask: int32 [2, 1024, 1024], P('level', ('patch', 'sub')), may hold values 0 or 1
- adjacency: int32 [2, 4, 4], P('level'), may hold values from -1 to 3, as said below
- nest_gain: float32 [2, 8192], P(None, ('patch', 'sub')), may hold values from 0.75 to 1
- nest_index: int32 [2, 8192], P(None, ('patch', 'sub')), may hold values from 0 to 1023, as said below
Outputs:
- height_out: float32 [4, 1024, 1024], P(('parts', 'level'), ('patch', 'sub')), parts along dimension 0
- momenta_out: float32 [2, 4, 1024, 1024], P(None, ('parts', 'level'), ('patch', 'sub')), parts along dimension 1
The draws below stay inside these ranges and needn't reach their ends.
There are 2 independent parts, one for each index of `parts`. The reference program is written for one: setup_inputs(seed, part) draws one part's arguments, and reference() takes and returns one part's arrays. A program takes and returns all parts, laid end to end along the dimension named above; an argument that names none is the same for every part. Nothing has to cross between parts.
Inputs may be any that keep to these rules, and one draw needn't show every extreme that they name: `adjacency`: the patches of a level sit on a grid of cells in an order drawn from the seed; each row of a patch lists its grid neighbours, -1 at the grid's edge, and neighbour links are symmetric. `nest_index`: entries index a cell of the same half patch's strip, 1024 cells long.
All inputs are finite; a program needn't handle non-finite values. No bound on the sum of `wet_mask` on one device may be relied on, other than what follows from the above.
Results may differ from the reference program's by a relative error of at most 0.00002.
Values sent between devices are 32-bit elements; how exact they have to be, the bound alone decides.
A program may use at most 64 MiB of HBM per device.

```python
import math
import jax
import jax.numpy as jnp

BR = 128
COLS = 1024
STEPS = 2
LEVELS = 2
PATCHES = 4
ROWS = 256
TOTAL_ROWS = 1024
SEGS = 8


def level_links(key):
    gcols = 1 << (PATCHES.bit_length() - 1) // 2
    grows = PATCHES // gcols
    order = jax.random.permutation(key, PATCHES).astype(jnp.int32)
    places = jnp.arange(PATCHES, dtype=jnp.int32)
    row_of = places // gcols
    col_of = places % gcols
    none = jnp.full((PATCHES,), -1, jnp.int32)
    north_place = jnp.where(row_of > 0, places - gcols, none)
    south_place = jnp.where(row_of < grows - 1, places + gcols, none)
    west_place = jnp.where(col_of > 0, places - 1, none)
    east_place = jnp.where(col_of < gcols - 1, places + 1, none)
    stacked = jnp.stack([north_place, south_place, west_place, east_place], axis=1)
    named = jnp.where(stacked >= 0, order[jnp.clip(stacked, 0, PATCHES - 1)], -1)
    return jnp.zeros((PATCHES, 4), jnp.int32).at[order].set(named)


def draw_adjacency(key, part):
    keys = jax.random.split(jax.random.fold_in(key, 11), LEVELS)
    return jax.vmap(level_links)(keys)


def draw_nest_index(key, part):
    first, second = jax.random.split(jax.random.fold_in(key, 23))
    offsets = jax.random.randint(first, (LEVELS, SEGS, 1), 0, COLS)
    jitter = jax.random.randint(second, (LEVELS, SEGS, COLS), 0, 3)
    cells = jnp.arange(COLS, dtype=jnp.int32)[None, None, :]
    table = (3 * cells + offsets + jitter) % COLS
    return table.reshape(LEVELS, SEGS * COLS).astype(jnp.int32)


def set_ends(result, rng, low, largest):
    place = [jax.random.randint(jax.random.fold_in(rng, axis), (), 0, length) for axis, length in enumerate(result.shape)]
    longest = result.shape.index(max(result.shape))
    beside = place[:longest] + [(place[longest] + 1) % result.shape[longest]] + place[longest + 1:]
    return result.at[tuple(place)].set(low).at[tuple(beside)].set(largest)


def block_levels(rng, shape, shards, least, high):
    loudness = 1.0
    for dim, shards_of in shards:
        heights = jax.random.uniform(jax.random.fold_in(jax.random.fold_in(rng, 6), dim), (shards_of,), jnp.float32, least / len(shards), high / len(shards))
        loudness = loudness * jnp.repeat(jnp.exp(heights), shape[dim] // shards_of).reshape((-1,) + (1,) * (len(shape) - 1 - dim))
    return loudness


def centred(rng, extent, spread, most, cuts=(), kind=jnp.bfloat16):
    factor_of = block_levels(rng, extent, cuts, -0.22, 0.18) if cuts else 1.0
    entries = jax.random.normal(rng, extent, jnp.float32) * spread * factor_of
    return jnp.minimum(jnp.maximum(entries, -most), most).astype(kind)


def setup_inputs(seed: int = 0, part: int = 0) -> dict:
    arg_keys = jax.random.split(jax.random.key(seed), 8)
    part_splits = jax.random.split(jax.random.fold_in(arg_keys[7], part), 8)
    return {
        "adjoint_height": centred(part_splits[0], (LEVELS, TOTAL_ROWS, COLS), 1.0, 6.0, ((0, 2), (1, 8)), jnp.float32),
        "adjoint_momenta": centred(part_splits[1], (2, LEVELS, TOTAL_ROWS, COLS), 1.0, 6.0, ((1, 2), (2, 8)), jnp.float32),
        "depth": jnp.clip(0.2 + 0.8 * jax.random.uniform(arg_keys[2], (LEVELS, TOTAL_ROWS, COLS), jnp.float32) ** block_levels(arg_keys[2], (LEVELS, TOTAL_ROWS, COLS), ((0, 2), (1, 8)), -0.2, 0.2), 0.2, 1.0),
        "wet_mask": set_ends((jax.random.randint(arg_keys[3], (LEVELS, TOTAL_ROWS, COLS), 0, 4) < 3).astype(jnp.int32), jax.random.fold_in(arg_keys[3], 1), 0, 1),
        "adjacency": draw_adjacency(jax.random.fold_in(arg_keys[7], 71), part),
        "nest_gain": jnp.clip(jnp.exp(math.log(1.0) - 0.2876821 * jax.random.uniform(arg_keys[5], (LEVELS, SEGS * COLS), jnp.float32) ** block_levels(arg_keys[5], (LEVELS, SEGS * COLS), ((1, 8),), -0.2, 0.2)), 0.75, 1.0),
        "nest_index": draw_nest_index(jax.random.fold_in(arg_keys[7], 71), part),
    }


courant = 0.45


def neighbour(field, links, level_ids):
    picked = field[level_ids, jnp.clip(links, 0, PATCHES - 1)]
    return picked * (links >= 0).astype(jnp.float32)[:, :, None, None]


def reference(adjoint_height, adjoint_momenta, depth, wet_mask, adjacency, nest_gain, nest_index):
    shape4 = (LEVELS, PATCHES, ROWS, COLS)
    eta = adjoint_height.reshape(shape4)
    mom_row = adjoint_momenta[0].reshape(shape4)
    mom_col = adjoint_momenta[1].reshape(shape4)
    height = depth.reshape(shape4)
    wet = wet_mask.astype(jnp.float32).reshape(shape4)
    north = adjacency[:, :, 0]
    south = adjacency[:, :, 1]
    west = adjacency[:, :, 2]
    east = adjacency[:, :, 3]
    level_ids = jnp.arange(LEVELS)[:, None]
    gains = nest_gain.reshape(LEVELS, SEGS, COLS)
    tables = nest_index.reshape(LEVELS, SEGS, COLS)
    for step in range(STEPS):
        halves = eta.reshape(LEVELS, SEGS, BR, COLS)
        strips = halves[:, :, 0, :]
        flux = jnp.zeros((SEGS, COLS), jnp.float32)
        inflows = []
        for lev in range(LEVELS - 1, -1, -1):
            inflow = gains[lev] * jnp.take_along_axis(flux, tables[lev], axis=1)
            flux = inflow + strips[lev]
            inflows.insert(0, inflow)
        halves = halves.at[:, :, 0, :].add(jnp.stack(inflows))
        eta = halves.reshape(shape4)
        east_eta = jnp.concatenate([eta[..., 1:], neighbour(eta, east, level_ids)[..., :1]], axis=3)
        south_eta = jnp.concatenate([eta[:, :, 1:, :], neighbour(eta, south, level_ids)[:, :, :1, :]], axis=2)
        mom_row = wet * (mom_row - courant * (east_eta - eta))
        mom_col = wet * (mom_col - courant * (south_eta - eta))
        west_row = jnp.concatenate([neighbour(mom_row, west, level_ids)[..., -1:], mom_row[..., :-1]], axis=3)
        north_col = jnp.concatenate([neighbour(mom_col, north, level_ids)[:, :, -1:, :], mom_col[:, :, :-1, :]], axis=2)
        eta = wet * (eta - courant * height * ((mom_row - west_row) + (mom_col - north_col)))
    flat = (LEVELS, TOTAL_ROWS, COLS)
    return eta.reshape(flat), jnp.stack([mom_row.reshape(flat), mom_col.reshape(flat)])
```

```python
import functools

import jax
import jax.numpy as jnp
from jax import lax
from jax.experimental import pallas as pl
from jax.experimental.pallas import tpu as pltpu
from jax.sharding import PartitionSpec as P

STEPS = 2
COURANT = 0.45
LANES = 128
BLOCK = 8


def kernel(patches, levels, rows, cols,
           adj, eta_hbm, mom_hbm, depth_hbm, wet_hbm, gain_hbm, table_hbm,
           eta_out, mom_out,
           E, Pm, Q, H, W, gain_v, table_v, f8, idx8, gain8, tmp,
           sfirst, slast, scol, sinf, sew,
           rown, in_sems, out_sems, send_sems, recv_sems, own_sems, *landing):
    rfirst, rlast, rcol, rnbr, rew = (landing[n * STEPS:(n + 1) * STEPS] for n in range(5))
    patch = lax.axis_index("patch")
    level = lax.axis_index("level")
    half = lax.axis_index("sub")
    chunks = cols // LANES
    other = 1 - half

    loads = [
        pltpu.make_async_copy(eta_hbm.at[0], E.at[0:rows], in_sems.at[0]),
        pltpu.make_async_copy(mom_hbm.at[0, 0], Pm, in_sems.at[1]),
        pltpu.make_async_copy(mom_hbm.at[1, 0], Q.at[8:8 + rows], in_sems.at[2]),
        pltpu.make_async_copy(wet_hbm.at[0], W, in_sems.at[3]),
        pltpu.make_async_copy(table_hbm, table_v, in_sems.at[4]),
        pltpu.make_async_copy(gain_hbm, gain_v, in_sems.at[5]),
        pltpu.make_async_copy(depth_hbm.at[0], H, in_sems.at[6]),
    ]
    for load in loads:
        load.start()

    barrier = pltpu.get_barrier_semaphore()

    def greet(d, h, lev):
        pl.semaphore_signal(barrier, inc=1, device_id={
            "patch": lax.rem(patch + d, patches), "sub": h, "level": lev},
            device_id_type=pl.DeviceIdType.MESH)

    for d in range(patches):
        if d:
            greet(d, half, level)
        greet(d, other, level)

    @pl.when(level > 0)
    def _():
        for d in range(patches):
            greet(d, half, level - 1)
            greet(d, other, level - 1)

    @pl.when(level < levels - 1)
    def _():
        for d in range(patches):
            greet(d, half, level + 1)
            greet(d, other, level + 1)

    sides = (level > 0).astype(jnp.int32) + (level < levels - 1).astype(jnp.int32)
    pl.semaphore_wait(barrier, 2 * patches - 1 + 2 * patches * sides)

    for load in loads[:6]:
        load.wait()

    lower = jnp.maximum(level - 1, 0)
    for c in range(chunks):
        lane = slice(c * LANES, (c + 1) * LANES)
        index, gain = table_v[0:1, lane], gain_v[0:1, lane]
        for lev in range(1, levels - 1):
            index = jnp.where(lower == lev, table_v[lev:lev + 1, lane], index)
            gain = jnp.where(lower == lev, gain_v[lev:lev + 1, lane], gain)
        idx8[c:c + 1, :] = index
        gain8[c:c + 1, :] = gain

    def remote(t, kind, src, buf, slot, d, h, lev):
        return pltpu.make_async_remote_copy(
            src_ref=src, dst_ref=buf, send_sem=send_sems.at[t, kind, d],
            recv_sem=recv_sems.at[t, kind, slot],
            device_id={"patch": lax.rem(patch + d, patches), "sub": h, "level": lev},
            device_id_type=pl.DeviceIdType.MESH)

    def slot_of(d):
        return lax.rem(patch + d, patches)

    def last_part(t):
        return slice(0, 2) if t == 0 else slice(t + 1, t + 2)

    def halo_copies(t, slot, d):
        col = remote(t, 0, scol.at[t], rcol[t].at[slot], slot, d, half, level)
        first = remote(t, 1, sfirst.at[t], rfirst[t].at[slot], slot, d, other, level)
        part = last_part(t)
        last = remote(t, 2, slast.at[part], rlast[t].at[slot], slot, d, other, level)
        return col, first, last

    def inf_copies(t, slot, d):
        beside = remote(t, 3, sinf.at[t], rnbr[t].at[slot], slot, d, other, lower)
        ends = remote(t, 4, sew.at[t], rew[t].at[slot], slot, d, half, lower)
        return beside, ends

    def own_copy(t):
        return pltpu.make_async_remote_copy(
            src_ref=sinf.at[t], dst_ref=rown.at[t], send_sem=own_sems.at[t, 0],
            recv_sem=own_sems.at[t, 1], device_id={"level": lower},
            device_id_type=pl.DeviceIdType.MESH)

    def send_inflow(t):
        for c in range(chunks):
            f8[c:c + 1, :] = E[0:1, c * LANES:(c + 1) * LANES]
        index = idx8[...]
        inside = jnp.bitwise_and(index, LANES - 1)
        which = lax.shift_right_logical(index, 7)
        picked = jnp.zeros((chunks, LANES), jnp.float32)
        for c in range(chunks):
            source = jnp.broadcast_to(f8[c:c + 1, :], (chunks, LANES))
            got = jnp.take_along_axis(source, inside, axis=1, mode="promise_in_bounds")
            picked = jnp.where(which == c, got, picked)
        inflow = gain8[...] * picked
        sinf[t] = inflow
        own_copy(t).start()
        sew[t, 0:1, :] = inflow[0:1, :]
        sew[t, 1:2, :] = pltpu.roll(inflow[chunks - 1:chunks, :], 1, 1)
        for d in range(patches):
            beside, ends = inf_copies(t, patch, d)

            @pl.when(half == (1 if d == 0 else 0))
            def _():
                beside.start()
            if d:
                ends.start()

    def inflow_waits(t):
        for d in range(patches):
            beside, ends = inf_copies(t, slot_of(d), d)

            @pl.when(half == (0 if d == 0 else 1))
            def _():
                beside.wait_recv()
            if d:
                ends.wait_recv()

    def inflow_send_waits(t):
        own_copy(t).wait_send()
        for d in range(patches):
            beside, ends = inf_copies(t, patch, d)

            @pl.when(half == (1 if d == 0 else 0))
            def _():
                beside.wait_send()
            if d:
                ends.wait_send()

    def each_halo(t, first_when, last_when, act, sending):
        for d in range(patches):
            col, first, last = halo_copies(t, patch if sending else slot_of(d), d)

            @pl.when(half == (first_when if d == 0 else 1 - first_when))
            def _():
                act(first)

            @pl.when(half == (last_when if d == 0 else 1 - last_when))
            def _():
                act(last)
            if d:
                act(col)

    north = adj[0, patch, 0]
    south = adj[0, patch, 1]
    west = adj[0, patch, 2]
    east = adj[0, patch, 3]
    south_ok = jnp.logical_or(half == 0, south >= 0)
    north_ok = jnp.logical_or(half == 1, north >= 0)
    south_at = jnp.where(half == 0, patch, jnp.maximum(south, 0))
    north_at = jnp.where(half == 1, patch, jnp.maximum(north, 0))
    west_at = jnp.maximum(west, 0)
    east_at = jnp.maximum(east, 0)
    finer = level < levels - 1
    lane_ids = lax.broadcasted_iota(jnp.int32, (rows, LANES), 1)
    first_lane = lax.broadcasted_iota(jnp.int32, (1, LANES), 1) == 0
    wide_ids = lax.broadcasted_iota(jnp.int32, (BLOCK, cols), 1)
    tail = slice(cols - LANES, cols)
    end = rows - 1

    for t in range(STEPS):
        @pl.when(level == levels - 1)
        def _():
            send_inflow(t)

        sfirst[t] = E[0:1, :]
        wet_row = W[end:rows, :].astype(jnp.float32)
        slast[t + 1] = wet_row * (Q[8 + end:8 + rows, :] + COURANT * E[end:rows, :])
        if t == 0:
            slast[0] = wet_row
        wet_tail = W[:, tail].astype(jnp.float32)
        share = wet_tail * (Pm[:, tail] + COURANT * E[0:rows, tail])
        mixed = jnp.where(lane_ids == 0, E[0:rows, 0:LANES],
                          jnp.where(lane_ids == 1, pltpu.roll(share, 2, 1),
                                    pltpu.roll(wet_tail, 3, 1)))
        scol[t] = jnp.transpose(mixed)[0:8, :]
        each_halo(t, 1, 0, lambda copy: copy.start(), True)

        @pl.when(finer)
        def _():
            own_copy(t).wait_recv()
            for c in range(chunks):
                lane = slice(c * LANES, (c + 1) * LANES)
                E[0:1, lane] += rown[t, c:c + 1, :]

        if levels > 2:
            @pl.when(jnp.logical_and(level > 0, level < levels - 1))
            def _():
                send_inflow(t)

        each_halo(t, 0, 1, lambda copy: copy.wait_recv(), False)

        @pl.when(finer)
        def _():
            inflow_waits(t)

        east_row = rcol[t][east_at][0:1, :]
        east_row += jnp.where(jnp.logical_and(first_lane, finer), rew[t][east_at][0:1, :], 0.0)
        west_cols = rcol[t][west_at]
        share = west_cols[1:2, :]
        wet_w = west_cols[2:3, :]
        share += jnp.where(jnp.logical_and(first_lane, finer),
                           COURANT * wet_w * rew[t][west_at][1:2, :], 0.0)
        tmp[0:1, :] = jnp.where(east >= 0, east_row, 0.0)
        tmp[1:2, :] = jnp.where(west >= 0, share, 0.0)
        tmp[2:3, :] = jnp.where(west >= 0, wet_w, 0.0)
        halo = jnp.transpose(tmp[...])
        beside = rnbr[t][south_at]
        below = rfirst[t][south_at]
        for c in range(chunks):
            lane = slice(c * LANES, (c + 1) * LANES)
            value = below[:, lane] + jnp.where(finer, beside[c:c + 1, :], 0.0)
            E[rows:rows + 1, lane] = jnp.where(south_ok, value, 0.0)
        share_n = rlast[t][north_at, 1 if t == 0 else 0]
        wet_n = rlast[0][north_at, 0]
        Q[7:8, :] = jnp.where(north_ok, share_n - COURANT * wet_n * E[0:1, :], 0.0)
        if t == 0:
            loads[6].wait()

        for r in range(0, rows, BLOCK):
            span = slice(r, r + BLOCK)
            e = E[span, :]
            wet = W[span, :].astype(jnp.float32)
            e_south = E[r + 1:r + 1 + BLOCK, :]
            e_east = jnp.where(wide_ids == cols - 1, halo[span, 0:1], pltpu.roll(e, cols - 1, 1))
            p = wet * (Pm[span, :] - COURANT * (e_east - e))
            q = wet * (Q[8 + r:16 + r, :] - COURANT * (e_south - e))
            p_edge = halo[span, 1:2] - COURANT * halo[span, 2:3] * e[:, 0:1]
            p_west = jnp.where(wide_ids == 0, p_edge, pltpu.roll(p, 1, 1))
            Pm[span, :] = p
            Q[8 + r:16 + r, :] = q
            q_north = Q[7 + r:15 + r, :]
            E[span, :] = wet * (e - COURANT * H[span, :] * ((p - p_west) + (q - q_north)))

    stores = [
        pltpu.make_async_copy(E.at[0:rows], eta_out.at[0], out_sems.at[0]),
        pltpu.make_async_copy(Pm, mom_out.at[0, 0], out_sems.at[1]),
        pltpu.make_async_copy(Q.at[8:8 + rows], mom_out.at[1, 0], out_sems.at[2]),
    ]
    for store in stores:
        store.start()
    for t in range(STEPS):
        each_halo(t, 1, 0, lambda copy: copy.wait_send(), True)

        @pl.when(level > 0)
        def _():
            inflow_send_waits(t)
    for store in stores:
        store.wait()


def body(mesh, adjoint_height, adjoint_momenta, depth, wet_mask, adjacency, nest_gain, nest_index):
    patches, levels = mesh.shape["patch"], mesh.shape["level"]
    rows, cols = adjoint_height.shape[1:]
    chunks = cols // LANES
    f32 = jnp.float32
    anywhere = pl.BlockSpec(memory_space=pl.ANY)
    v = pltpu.VMEM
    scratch = [
        v((rows + 8, cols), f32), v((rows, cols), f32), v((rows + 8, cols), f32),
        v((rows, cols), f32), v((rows, cols), jnp.int32),
        v(nest_gain.shape, f32), v(nest_index.shape, jnp.int32),
        v((chunks, LANES), f32), v((chunks, LANES), jnp.int32), v((chunks, LANES), f32),
        v((8, LANES), f32),
        v((STEPS, 1, cols), f32), v((STEPS + 1, 1, cols), f32), v((STEPS, 8, LANES), f32),
        v((STEPS, chunks, LANES), f32), v((STEPS, 2, LANES), f32),
        v((STEPS, chunks, LANES), f32),
        pltpu.SemaphoreType.DMA((7,)), pltpu.SemaphoreType.DMA((3,)),
        pltpu.SemaphoreType.DMA((STEPS, 5, patches)), pltpu.SemaphoreType.DMA((STEPS, 5, patches)),
        pltpu.SemaphoreType.DMA((STEPS, 2)),
    ]
    scratch += [v((patches, 1, cols), f32)] * STEPS
    scratch += [v((patches, 2 if t == 0 else 1, 1, cols), f32) for t in range(STEPS)]
    scratch += [v((patches, 8, LANES), f32)] * STEPS
    scratch += [v((patches, chunks, LANES), f32)] * STEPS
    scratch += [v((patches, 2, LANES), f32)] * STEPS
    return pl.pallas_call(
        functools.partial(kernel, patches, levels, rows, cols),
        out_shape=(jax.ShapeDtypeStruct(adjoint_height.shape, f32),
                   jax.ShapeDtypeStruct(adjoint_momenta.shape, f32)),
        in_specs=[pl.BlockSpec(memory_space=pltpu.SMEM)] + [anywhere] * 6,
        out_specs=(anywhere, anywhere),
        scratch_shapes=scratch,
        compiler_params=pltpu.CompilerParams(collective_id=0, has_side_effects=True),
    )(adjacency, adjoint_height, adjoint_momenta, depth, wet_mask, nest_gain, nest_index)


def solution(mesh):
    in_specs = (
        P(("parts", "level"), ("patch", "sub"), None),
        P(None, ("parts", "level"), ("patch", "sub"), None),
        P("level", ("patch", "sub"), None),
        P("level", ("patch", "sub"), None),
        P("level", None, None),
        P(None, ("patch", "sub")),
        P(None, ("patch", "sub")),
    )
    out_specs = (
        P(("parts", "level"), ("patch", "sub"), None),
        P(None, ("parts", "level"), ("patch", "sub"), None),
    )
    return jax.shard_map(functools.partial(body, mesh), mesh=mesh, in_specs=in_specs,
                         out_specs=out_specs, check_vma=False)
```

```python
import functools

import jax
import jax.numpy as jnp
from jax import lax
from jax.experimental import pallas as pl
from jax.experimental.pallas import tpu as pltpu
from jax.sharding import PartitionSpec as P

STEPS = 2
COURANT = 0.45
LANES = 128
BLOCK = 8
GROUP = 32


def advance(r, E, Pm, Q, H, W, halo, E_to, P_to, Q_to):
    cols = Pm.shape[1]
    lane_ids = lax.broadcasted_iota(jnp.int32, (BLOCK, cols), 1)
    span = slice(r, r + BLOCK)
    e = E[span, :]
    wet = W[span, :].astype(jnp.float32)
    e_south = E[r + 1:r + 1 + BLOCK, :]
    e_east = pltpu.roll(e, cols - 1, 1)
    if halo is not None:
        e_east = jnp.where(lane_ids == cols - 1, halo[span, 0:1], e_east)
    p = wet * (Pm[span, :] - COURANT * (e_east - e))
    q = wet * (Q[8 + r:16 + r, :] - COURANT * (e_south - e))
    p_west = pltpu.roll(p, 1, 1)
    if halo is not None:
        p_edge = halo[span, 1:2] - COURANT * halo[span, 2:3] * e[:, 0:1]
        p_west = jnp.where(lane_ids == 0, p_edge, p_west)
    P_to[span, :] = p
    Q_to[8 + r:16 + r, :] = q
    q_north = Q_to[7 + r:15 + r, :]
    E_to[span, :] = wet * (e - COURANT * H[span, :] * ((p - p_west) + (q - q_north)))


def finish(rows, E, Pm, Q, H, W, halo, eta_out, mom_out, E2, P2, Q2, sems):
    Q2[7:8, :] = Q[7:8, :]
    stores = []
    edges = halo[...]
    for r in range(0, rows, BLOCK):
        advance(r, E, Pm, Q, H, W, edges, E2, P2, Q2)
        if (r + BLOCK) % GROUP == 0:
            g = r // GROUP
            at = slice(g * GROUP, (g + 1) * GROUP)
            for n, (src, dst) in enumerate((
                    (P2.at[at], mom_out.at[0, 0, at]),
                    (Q2.at[8 + g * GROUP:8 + (g + 1) * GROUP], mom_out.at[1, 0, at]),
                    (E2.at[at], eta_out.at[0, at]))):
                store = pltpu.make_async_copy(src, dst, sems.at[g, n])
                store.start()
                stores.append(store)
    for store in stores:
        store.wait()


def exchange(patches, levels, rows, cols,
             adj, eta_hbm, mom_hbm, depth_hbm, wet_hbm, gain_hbm, table_hbm,
             E1, P1, Q1, H, W, halo_out,
             E0, P0, Q0, gain_v, table_v, f8, idx8, gain8, tmp,
             sfirst, slast, scol, sinf, sew,
             rown, in_sems, send_sems, recv_sems, own_sems, *landing):
    rfirst, rlast, rcol, rnbr, rew = (landing[n * STEPS:(n + 1) * STEPS] for n in range(5))
    fields = ((E0, P0, Q0), (E1, P1, Q1))
    patch = lax.axis_index("patch")
    level = lax.axis_index("level")
    half = lax.axis_index("sub")
    chunks = cols // LANES
    other = 1 - half

    loads = [
        pltpu.make_async_copy(eta_hbm.at[0], E0.at[0:rows], in_sems.at[0]),
        pltpu.make_async_copy(mom_hbm.at[0, 0], P0, in_sems.at[1]),
        pltpu.make_async_copy(mom_hbm.at[1, 0], Q0.at[8:8 + rows], in_sems.at[2]),
        pltpu.make_async_copy(wet_hbm.at[0], W, in_sems.at[3]),
        pltpu.make_async_copy(table_hbm, table_v, in_sems.at[4]),
        pltpu.make_async_copy(gain_hbm, gain_v, in_sems.at[5]),
        pltpu.make_async_copy(depth_hbm.at[0], H, in_sems.at[6]),
    ]
    for load in loads:
        load.start()

    barrier = pltpu.get_barrier_semaphore()

    def greet(d, h, lev):
        pl.semaphore_signal(barrier, inc=1, device_id={
            "patch": lax.rem(patch + d, patches), "sub": h, "level": lev},
            device_id_type=pl.DeviceIdType.MESH)

    for d in range(patches):
        if d:
            greet(d, half, level)
        greet(d, other, level)

    @pl.when(level > 0)
    def _():
        for d in range(patches):
            greet(d, half, level - 1)
            greet(d, other, level - 1)

    @pl.when(level < levels - 1)
    def _():
        for d in range(patches):
            greet(d, half, level + 1)
            greet(d, other, level + 1)

    for load in loads[:6]:
        load.wait()

    lower = jnp.maximum(level - 1, 0)
    for c in range(chunks):
        lane = slice(c * LANES, (c + 1) * LANES)
        index, gain = table_v[0:1, lane], gain_v[0:1, lane]
        for lev in range(1, levels - 1):
            index = jnp.where(lower == lev, table_v[lev:lev + 1, lane], index)
            gain = jnp.where(lower == lev, gain_v[lev:lev + 1, lane], gain)
        idx8[c:c + 1, :] = index
        gain8[c:c + 1, :] = gain

    def remote(t, kind, src, buf, slot, d, h, lev):
        return pltpu.make_async_remote_copy(
            src_ref=src, dst_ref=buf, send_sem=send_sems.at[t, kind, d],
            recv_sem=recv_sems.at[t, kind, slot],
            device_id={"patch": lax.rem(patch + d, patches), "sub": h, "level": lev},
            device_id_type=pl.DeviceIdType.MESH)

    def slot_of(d):
        return lax.rem(patch + d, patches)

    def last_part(t):
        return slice(0, 2) if t == 0 else slice(t + 1, t + 2)

    def halo_copies(t, slot, d):
        col = remote(t, 0, scol.at[t], rcol[t].at[slot], slot, d, half, level)
        first = remote(t, 1, sfirst.at[t], rfirst[t].at[slot], slot, d, other, level)
        part = last_part(t)
        last = remote(t, 2, slast.at[part], rlast[t].at[slot], slot, d, other, level)
        return col, first, last

    def inf_copies(t, slot, d):
        beside = remote(t, 3, sinf.at[t], rnbr[t].at[slot], slot, d, other, lower)
        ends = remote(t, 4, sew.at[t], rew[t].at[slot], slot, d, half, lower)
        return beside, ends

    def own_copy(t):
        return pltpu.make_async_remote_copy(
            src_ref=sinf.at[t], dst_ref=rown.at[t], send_sem=own_sems.at[t, 0],
            recv_sem=own_sems.at[t, 1], device_id={"level": lower},
            device_id_type=pl.DeviceIdType.MESH)

    def make_inflow(t):
        E = fields[t][0]
        for c in range(chunks):
            f8[c:c + 1, :] = E[0:1, c * LANES:(c + 1) * LANES]
        index = idx8[...]
        inside = jnp.bitwise_and(index, LANES - 1)
        which = lax.shift_right_logical(index, 7)
        picked = jnp.zeros((chunks, LANES), jnp.float32)
        for c in range(chunks):
            source = jnp.broadcast_to(f8[c:c + 1, :], (chunks, LANES))
            got = jnp.take_along_axis(source, inside, axis=1, mode="promise_in_bounds")
            picked = jnp.where(which == c, got, picked)
        inflow = gain8[...] * picked
        sinf[t] = inflow
        sew[t, 0:1, :] = inflow[0:1, :]
        sew[t, 1:2, :] = pltpu.roll(inflow[chunks - 1:chunks, :], 1, 1)

    def send_inflow(t):
        own_copy(t).start()
        for d in range(patches):
            beside, ends = inf_copies(t, patch, d)

            @pl.when(half == (1 if d == 0 else 0))
            def _():
                beside.start()
            if d:
                ends.start()

    def inflow_waits(t):
        for d in range(patches):
            beside, ends = inf_copies(t, slot_of(d), d)

            @pl.when(half == (0 if d == 0 else 1))
            def _():
                beside.wait_recv()
            if d:
                ends.wait_recv()

    def inflow_send_waits(t):
        own_copy(t).wait_send()
        for d in range(patches):
            beside, ends = inf_copies(t, patch, d)

            @pl.when(half == (1 if d == 0 else 0))
            def _():
                beside.wait_send()
            if d:
                ends.wait_send()

    def each_halo(t, first_when, last_when, act, sending):
        for d in range(patches):
            col, first, last = halo_copies(t, patch if sending else slot_of(d), d)

            @pl.when(half == (first_when if d == 0 else 1 - first_when))
            def _():
                act(first)

            @pl.when(half == (last_when if d == 0 else 1 - last_when))
            def _():
                act(last)
            if d:
                act(col)

    north = adj[0, patch, 0]
    south = adj[0, patch, 1]
    west = adj[0, patch, 2]
    east = adj[0, patch, 3]
    south_ok = jnp.logical_or(half == 0, south >= 0)
    north_ok = jnp.logical_or(half == 1, north >= 0)
    south_at = jnp.where(half == 0, patch, jnp.maximum(south, 0))
    north_at = jnp.where(half == 1, patch, jnp.maximum(north, 0))
    west_at = jnp.maximum(west, 0)
    east_at = jnp.maximum(east, 0)
    finer = level < levels - 1
    lane_ids = lax.broadcasted_iota(jnp.int32, (rows, LANES), 1)
    first_lane = lax.broadcasted_iota(jnp.int32, (1, LANES), 1) == 0
    tail = slice(cols - LANES, cols)
    end = rows - 1

    def make_messages(t):
        E, Pm, Q = fields[t]

        @pl.when(level == levels - 1)
        def _():
            make_inflow(t)

        sfirst[t] = E[0:1, :]
        wet_row = W[end:rows, :].astype(jnp.float32)
        slast[t + 1] = wet_row * (Q[8 + end:8 + rows, :] + COURANT * E[end:rows, :])
        if t == 0:
            slast[0] = wet_row
        wet_tail = W[:, tail].astype(jnp.float32)
        share = wet_tail * (Pm[:, tail] + COURANT * E[0:rows, tail])
        mixed = jnp.where(lane_ids == 0, E[0:rows, 0:LANES],
                          jnp.where(lane_ids == 1, pltpu.roll(share, 2, 1),
                                    pltpu.roll(wet_tail, 3, 1)))
        scol[t] = jnp.transpose(mixed)[0:8, :]

    def send_messages(t):
        @pl.when(level == levels - 1)
        def _():
            send_inflow(t)

        each_halo(t, 1, 0, lambda copy: copy.start(), True)

    def receive(t):
        E, Pm, Q = fields[t]

        @pl.when(finer)
        def _():
            own_copy(t).wait_recv()
            for c in range(chunks):
                lane = slice(c * LANES, (c + 1) * LANES)
                E[0:1, lane] += rown[t, c:c + 1, :]

        if levels > 2:
            @pl.when(jnp.logical_and(level > 0, level < levels - 1))
            def _():
                make_inflow(t)
                send_inflow(t)

        each_halo(t, 0, 1, lambda copy: copy.wait_recv(), False)

        @pl.when(finer)
        def _():
            inflow_waits(t)

        east_row = rcol[t][east_at][0:1, :]
        east_row += jnp.where(jnp.logical_and(first_lane, finer), rew[t][east_at][0:1, :], 0.0)
        west_cols = rcol[t][west_at]
        share = west_cols[1:2, :]
        wet_w = west_cols[2:3, :]
        share += jnp.where(jnp.logical_and(first_lane, finer),
                           COURANT * wet_w * rew[t][west_at][1:2, :], 0.0)
        tmp[0:1, :] = jnp.where(east >= 0, east_row, 0.0)
        tmp[1:2, :] = jnp.where(west >= 0, share, 0.0)
        tmp[2:3, :] = jnp.where(west >= 0, wet_w, 0.0)
        beside = rnbr[t][south_at]
        below = rfirst[t][south_at]
        for c in range(chunks):
            lane = slice(c * LANES, (c + 1) * LANES)
            value = below[:, lane] + jnp.where(finer, beside[c:c + 1, :], 0.0)
            E[rows:rows + 1, lane] = jnp.where(south_ok, value, 0.0)
        share_n = rlast[t][north_at, 1 if t == 0 else 0]
        wet_n = rlast[0][north_at, 0]
        Q_to = Q1
        Q_to[7:8, :] = jnp.where(north_ok, share_n - COURANT * wet_n * E[0:1, :], 0.0)
        return jnp.transpose(tmp[...])

    make_messages(0)
    sides = (level > 0).astype(jnp.int32) + (level < levels - 1).astype(jnp.int32)
    pl.semaphore_wait(barrier, 2 * patches - 1 + 2 * patches * sides)
    send_messages(0)
    loads[6].wait()
    for r in range(0, rows - BLOCK, BLOCK):
        advance(r, E0, P0, Q0, H, W, None, E1, P1, Q1)
    halo = receive(0)
    for r in (0, rows - BLOCK):
        advance(r, E0, P0, Q0, H, W, None, E1, P1, Q1)
    head = slice(0, LANES)
    e = E0[0:rows, head]
    wet = W[:, head].astype(jnp.float32)
    p_edge = halo[:, 1:2] - COURANT * halo[:, 2:3] * e[:, 0:1]
    across = Q1[8:8 + rows, head] - Q1[7:7 + rows, head]
    fixed = wet * (e - COURANT * H[:, head] * ((P1[:, head] - p_edge) + across))
    E1[0:rows, head] = jnp.where(lane_ids == 0, fixed, E1[0:rows, head])
    e = E0[0:rows, tail]
    wet = W[:, tail].astype(jnp.float32)
    p = wet * (P0[:, tail] - COURANT * (halo[:, 0:1] - e))
    p = jnp.where(lane_ids == LANES - 1, p, P1[:, tail])
    P1[:, tail] = p
    across = Q1[8:8 + rows, tail] - Q1[7:7 + rows, tail]
    fixed = wet * (e - COURANT * H[:, tail] * ((p - pltpu.roll(p, 1, 1)) + across))
    E1[0:rows, tail] = jnp.where(lane_ids == LANES - 1, fixed, E1[0:rows, tail])

    make_messages(1)
    send_messages(1)
    halo_out[...] = receive(1)
    for t in range(STEPS):
        each_halo(t, 1, 0, lambda copy: copy.wait_send(), True)

        @pl.when(level > 0)
        def _():
            inflow_send_waits(t)


def body(mesh, adjoint_height, adjoint_momenta, depth, wet_mask, adjacency, nest_gain, nest_index):
    patches, levels = mesh.shape["patch"], mesh.shape["level"]
    rows, cols = adjoint_height.shape[1:]
    chunks = cols // LANES
    f32 = jnp.float32
    anywhere = pl.BlockSpec(memory_space=pl.ANY)
    v = pltpu.VMEM
    dma = pltpu.SemaphoreType.DMA
    scratch = [
        v((rows + 8, cols), f32), v((rows, cols), f32), v((rows + 8, cols), f32),
        v(nest_gain.shape, f32), v(nest_index.shape, jnp.int32),
        v((chunks, LANES), f32), v((chunks, LANES), jnp.int32), v((chunks, LANES), f32),
        v((8, LANES), f32),
        v((STEPS, 1, cols), f32), v((STEPS + 1, 1, cols), f32), v((STEPS, 8, LANES), f32),
        v((STEPS, chunks, LANES), f32), v((STEPS, 2, LANES), f32),
        v((STEPS, chunks, LANES), f32),
        dma((7,)), dma((STEPS, 5, patches)), dma((STEPS, 5, patches)), dma((STEPS, 2)),
    ]
    scratch += [v((patches, 1, cols), f32)] * STEPS
    scratch += [v((patches, 2 if t == 0 else 1, 1, cols), f32) for t in range(STEPS)]
    scratch += [v((patches, 8, LANES), f32)] * STEPS
    scratch += [v((patches, chunks, LANES), f32)] * STEPS
    scratch += [v((patches, 2, LANES), f32)] * STEPS
    here = pl.BlockSpec(memory_space=pltpu.VMEM)
    state = pl.pallas_call(
        functools.partial(exchange, patches, levels, rows, cols),
        out_shape=(v((rows + 8, cols), f32), v((rows, cols), f32), v((rows + 8, cols), f32),
                   v((rows, cols), f32), v((rows, cols), jnp.int32), v((rows, 8), f32)),
        in_specs=[pl.BlockSpec(memory_space=pltpu.SMEM)] + [anywhere] * 6,
        out_specs=(here,) * 6,
        scratch_shapes=scratch,
        compiler_params=pltpu.CompilerParams(collective_id=0, has_side_effects=True),
    )(adjacency, adjoint_height, adjoint_momenta, depth, wet_mask, nest_gain, nest_index)
    state = [pltpu.with_memory_space_constraint(x, pltpu.VMEM) for x in state]
    return pl.pallas_call(
        functools.partial(finish, rows),
        out_shape=(jax.ShapeDtypeStruct(adjoint_height.shape, f32),
                   jax.ShapeDtypeStruct(adjoint_momenta.shape, f32)),
        in_specs=[here] * 6,
        out_specs=(anywhere, anywhere),
        scratch_shapes=[v((rows + 8, cols), f32), v((rows, cols), f32), v((rows + 8, cols), f32),
                        dma((rows // GROUP, 3))],
    )(*state)


def solution(mesh):
    in_specs = (
        P(("parts", "level"), ("patch", "sub"), None),
        P(None, ("parts", "level"), ("patch", "sub"), None),
        P("level", ("patch", "sub"), None),
        P("level", ("patch", "sub"), None),
        P("level", None, None),
        P(None, ("patch", "sub")),
        P(None, ("patch", "sub")),
    )
    out_specs = (
        P(("parts", "level"), ("patch", "sub"), None),
        P(None, ("parts", "level"), ("patch", "sub"), None),
    )
    return jax.shard_map(functools.partial(body, mesh), mesh=mesh, in_specs=in_specs,
                         out_specs=out_specs, check_vma=False)
```

```python
import functools

import jax
import jax.numpy as jnp
from jax import lax
from jax.experimental import pallas as pl
from jax.experimental.pallas import tpu as pltpu
from jax.sharding import PartitionSpec as P

STEPS = 2
COURANT = 0.45
LANES = 128
BLOCK = 8


def advance(r, E, Pm, Q, H, W, halo, E_to, P_to, Q_to):
    cols = Pm.shape[1]
    lane_ids = lax.broadcasted_iota(jnp.int32, (BLOCK, cols), 1)
    span = slice(r, r + BLOCK)
    e = E[span, :]
    wet = W[span, :].astype(jnp.float32)
    e_south = E[r + 1:r + 1 + BLOCK, :]
    e_east = pltpu.roll(e, cols - 1, 1)
    if halo is not None:
        e_east = jnp.where(lane_ids == cols - 1, halo[span, 0:1], e_east)
    p = wet * (Pm[span, :] - COURANT * (e_east - e))
    q = wet * (Q[8 + r:16 + r, :] - COURANT * (e_south - e))
    p_west = pltpu.roll(p, 1, 1)
    if halo is not None:
        p_edge = halo[span, 1:2] - COURANT * halo[span, 2:3] * e[:, 0:1]
        p_west = jnp.where(lane_ids == 0, p_edge, p_west)
    P_to[span, :] = p
    Q_to[8 + r:16 + r, :] = q
    q_north = Q_to[7 + r:15 + r, :]
    E_to[span, :] = wet * (e - COURANT * H[span, :] * ((p - p_west) + (q - q_north)))


def finish(rows, E, Pm, Q, H, W, halo, E2, P2, Q2, eta_out, mom_out, Ef, Pf, Qf, sems):
    cols = Pm.shape[1]
    end = rows - BLOCK
    mid = slice(BLOCK, end)
    head, tail = slice(0, LANES), slice(cols - LANES, cols)
    before, inner = slice(0, cols - LANES), slice(LANES, cols - LANES)
    stores = []

    def store(src, dst):
        copy = pltpu.make_async_copy(src, dst, sems.at[len(stores)])
        copy.start()
        stores.append(copy)

    eta_to, row_to, col_to = eta_out.at[0], mom_out.at[0, 0], mom_out.at[1, 0]
    store(Q2.at[BLOCK + 8:end + 8], col_to.at[mid])
    store(P2.at[mid, before], row_to.at[mid, before])
    store(E2.at[mid, inner], eta_to.at[mid, inner])
    edges = halo[...]
    lane_ids = lax.broadcasted_iota(jnp.int32, (end - BLOCK, LANES), 1)

    across = Q2[BLOCK + 8:end + 8, head] - Q2[BLOCK + 7:end + 7, head]
    e = E[mid, head]
    wet = W[mid, head].astype(jnp.float32)
    p_edge = edges[mid, 1:2] - COURANT * edges[mid, 2:3] * e[:, 0:1]
    fixed = wet * (e - COURANT * H[mid, head] * ((P2[mid, head] - p_edge) + across))
    Ef[mid, head] = jnp.where(lane_ids == 0, fixed, E2[mid, head])
    store(Ef.at[mid, head], eta_to.at[mid, head])

    across = Q2[BLOCK + 8:end + 8, tail] - Q2[BLOCK + 7:end + 7, tail]
    e = E[mid, tail]
    wet = W[mid, tail].astype(jnp.float32)
    p = wet * (Pm[mid, tail] - COURANT * (edges[mid, 0:1] - e))
    p = jnp.where(lane_ids == LANES - 1, p, P2[mid, tail])
    Pf[mid, tail] = p
    store(Pf.at[mid, tail], row_to.at[mid, tail])
    fixed = wet * (e - COURANT * H[mid, tail] * ((p - pltpu.roll(p, 1, 1)) + across))
    Ef[mid, tail] = jnp.where(lane_ids == LANES - 1, fixed, E2[mid, tail])
    store(Ef.at[mid, tail], eta_to.at[mid, tail])

    for r in (0, end):
        Qf[7 + r:8 + r, :] = (Q if r == 0 else Q2)[7 + r:8 + r, :]
        advance(r, E, Pm, Q, H, W, edges, Ef, Pf, Qf)
        at = slice(r, r + BLOCK)
        store(Pf.at[at], row_to.at[at])
        store(Qf.at[8 + r:16 + r], col_to.at[at])
        store(Ef.at[at], eta_to.at[at])
    for copy in stores:
        copy.wait()


def exchange(patches, levels, rows, cols,
             adj_hbm, eta_hbm, mom_hbm, depth_hbm, wet_hbm, gain_hbm, table_hbm,
             E1, P1, Q1, H, W, halo_out, E2, P2, Q2,
             adj, E0, P0, Q0, gain_v, table_v, f8, idx8, gain8, tmp,
             sfirst, slast, scol, sinf, sew,
             rown, in_sems, send_sems, recv_sems, own_sems, *landing):
    rfirst, rlast, rcol, rnbr, rew = (landing[n * STEPS:(n + 1) * STEPS] for n in range(5))
    fields = ((E0, P0, Q0), (E1, P1, Q1))
    patch = lax.axis_index("patch")
    level = lax.axis_index("level")
    half = lax.axis_index("sub")
    chunks = cols // LANES
    other = 1 - half

    loads = [
        pltpu.make_async_copy(eta_hbm.at[0], E0.at[0:rows], in_sems.at[0]),
        pltpu.make_async_copy(mom_hbm.at[0, 0], P0, in_sems.at[1]),
        pltpu.make_async_copy(mom_hbm.at[1, 0], Q0.at[8:8 + rows], in_sems.at[2]),
        pltpu.make_async_copy(wet_hbm.at[0], W, in_sems.at[3]),
        pltpu.make_async_copy(table_hbm, table_v, in_sems.at[4]),
        pltpu.make_async_copy(gain_hbm, gain_v, in_sems.at[5]),
        pltpu.make_async_copy(adj_hbm, adj, in_sems.at[6]),
        pltpu.make_async_copy(depth_hbm.at[0], H, in_sems.at[7]),
    ]
    barrier = pltpu.get_barrier_semaphore()

    def greet(d, h, lev):
        pl.semaphore_signal(barrier, inc=1, device_id={
            "patch": lax.rem(patch + d, patches), "sub": h, "level": lev},
            device_id_type=pl.DeviceIdType.MESH)

    for d in range(patches - 1, -1, -1):
        greet(d, other, level)
        if d:
            greet(d, half, level)

    @pl.when(level > 0)
    def _():
        for d in range(patches):
            greet(d, half, level - 1)
            greet(d, other, level - 1)

    @pl.when(level < levels - 1)
    def _():
        for d in range(patches):
            greet(d, half, level + 1)
            greet(d, other, level + 1)

    for load in loads:
        load.start()

    for load in loads[:7]:
        load.wait()

    lower = jnp.maximum(level - 1, 0)
    for c in range(chunks):
        lane = slice(c * LANES, (c + 1) * LANES)
        index, gain = table_v[0:1, lane], gain_v[0:1, lane]
        for lev in range(1, levels - 1):
            index = jnp.where(lower == lev, table_v[lev:lev + 1, lane], index)
            gain = jnp.where(lower == lev, gain_v[lev:lev + 1, lane], gain)
        idx8[c:c + 1, :] = index
        gain8[c:c + 1, :] = gain

    def remote(t, kind, src, buf, slot, d, h, lev):
        return pltpu.make_async_remote_copy(
            src_ref=src, dst_ref=buf, send_sem=send_sems.at[t, kind, d],
            recv_sem=recv_sems.at[t, kind, slot],
            device_id={"patch": lax.rem(patch + d, patches), "sub": h, "level": lev},
            device_id_type=pl.DeviceIdType.MESH)

    def slot_of(d):
        return lax.rem(patch + d, patches)

    def last_part(t):
        return slice(0, 2) if t == 0 else slice(t + 1, t + 2)

    def halo_copies(t, slot, d):
        col = remote(t, 0, scol.at[t], rcol[t].at[slot], slot, d, half, level)
        first = remote(t, 1, sfirst.at[t], rfirst[t].at[slot], slot, d, other, level)
        part = last_part(t)
        last = remote(t, 2, slast.at[part], rlast[t].at[slot], slot, d, other, level)
        return col, first, last

    def inf_copies(t, slot, d):
        beside = remote(t, 3, sinf.at[t], rnbr[t].at[slot], slot, d, other, lower)
        ends = remote(t, 4, sew.at[t], rew[t].at[slot], slot, d, half, lower)
        return beside, ends

    def own_copy(t):
        return pltpu.make_async_remote_copy(
            src_ref=sinf.at[t], dst_ref=rown.at[t], send_sem=own_sems.at[t, 0],
            recv_sem=own_sems.at[t, 1], device_id={"level": lower},
            device_id_type=pl.DeviceIdType.MESH)

    def make_inflow(t):
        E = fields[t][0]
        for c in range(chunks):
            f8[c:c + 1, :] = E[0:1, c * LANES:(c + 1) * LANES]
        index = idx8[...]
        inside = jnp.bitwise_and(index, LANES - 1)
        which = lax.shift_right_logical(index, 7)
        picked = jnp.zeros((chunks, LANES), jnp.float32)
        for c in range(chunks):
            source = jnp.broadcast_to(f8[c:c + 1, :], (chunks, LANES))
            got = jnp.take_along_axis(source, inside, axis=1, mode="promise_in_bounds")
            picked = jnp.where(which == c, got, picked)
        inflow = gain8[...] * picked
        sinf[t] = inflow
        sew[t, 0:1, :] = inflow[0:1, :]
        sew[t, 1:2, :] = pltpu.roll(inflow[chunks - 1:chunks, :], 1, 1)

    def send_inflow(t):
        own_copy(t).start()
        for d in range(patches):
            beside, ends = inf_copies(t, patch, d)

            @pl.when(half == (1 if d == 0 else 0))
            def _():
                beside.start()
            if d:
                ends.start()

    def inflow_waits(t):
        for d in range(patches):
            beside, ends = inf_copies(t, slot_of(d), d)

            @pl.when(half == (0 if d == 0 else 1))
            def _():
                beside.wait_recv()
            if d:
                ends.wait_recv()

    def inflow_send_waits(t):
        own_copy(t).wait_send()
        for d in range(patches):
            beside, ends = inf_copies(t, patch, d)

            @pl.when(half == (1 if d == 0 else 0))
            def _():
                beside.wait_send()
            if d:
                ends.wait_send()

    def each_halo(t, first_when, last_when, act, sending):
        for d in range(patches):
            col, first, last = halo_copies(t, patch if sending else slot_of(d), d)

            @pl.when(half == (first_when if d == 0 else 1 - first_when))
            def _():
                act(first)

            @pl.when(half == (last_when if d == 0 else 1 - last_when))
            def _():
                act(last)
            if d:
                act(col)

    north = adj[0, patch, 0]
    south = adj[0, patch, 1]
    west = adj[0, patch, 2]
    east = adj[0, patch, 3]
    south_ok = jnp.logical_or(half == 0, south >= 0)
    north_ok = jnp.logical_or(half == 1, north >= 0)
    south_at = jnp.where(half == 0, patch, jnp.maximum(south, 0))
    north_at = jnp.where(half == 1, patch, jnp.maximum(north, 0))
    west_at = jnp.maximum(west, 0)
    east_at = jnp.maximum(east, 0)
    finer = level < levels - 1
    lane_ids = lax.broadcasted_iota(jnp.int32, (rows, LANES), 1)
    first_lane = lax.broadcasted_iota(jnp.int32, (1, LANES), 1) == 0
    tail = slice(cols - LANES, cols)
    end = rows - 1

    def make_messages(t):
        E, Pm, Q = fields[t]

        @pl.when(level == levels - 1)
        def _():
            make_inflow(t)

        sfirst[t] = E[0:1, :]
        wet_row = W[end:rows, :].astype(jnp.float32)
        slast[t + 1] = wet_row * (Q[8 + end:8 + rows, :] + COURANT * E[end:rows, :])
        if t == 0:
            slast[0] = wet_row
        wet_tail = W[:, tail].astype(jnp.float32)
        share = wet_tail * (Pm[:, tail] + COURANT * E[0:rows, tail])
        mixed = jnp.where(lane_ids == 0, E[0:rows, 0:LANES],
                          jnp.where(lane_ids == 1, pltpu.roll(share, 2, 1),
                                    pltpu.roll(wet_tail, 3, 1)))
        scol[t] = jnp.transpose(mixed)[0:8, :]

    def send_messages(t):
        @pl.when(level == levels - 1)
        def _():
            send_inflow(t)

        each_halo(t, 1, 0, lambda copy: copy.start(), True)

    def receive(t):
        E, Pm, Q = fields[t]

        @pl.when(finer)
        def _():
            own_copy(t).wait_recv()
            for c in range(chunks):
                lane = slice(c * LANES, (c + 1) * LANES)
                E[0:1, lane] += rown[t, c:c + 1, :]

        if levels > 2:
            @pl.when(jnp.logical_and(level > 0, level < levels - 1))
            def _():
                make_inflow(t)
                send_inflow(t)

        each_halo(t, 0, 1, lambda copy: copy.wait_recv(), False)

        @pl.when(finer)
        def _():
            inflow_waits(t)

        east_row = rcol[t][east_at][0:1, :]
        east_row += jnp.where(jnp.logical_and(first_lane, finer), rew[t][east_at][0:1, :], 0.0)
        west_cols = rcol[t][west_at]
        share = west_cols[1:2, :]
        wet_w = west_cols[2:3, :]
        share += jnp.where(jnp.logical_and(first_lane, finer),
                           COURANT * wet_w * rew[t][west_at][1:2, :], 0.0)
        tmp[0:1, :] = jnp.where(east >= 0, east_row, 0.0)
        tmp[1:2, :] = jnp.where(west >= 0, share, 0.0)
        tmp[2:3, :] = jnp.where(west >= 0, wet_w, 0.0)
        beside = rnbr[t][south_at]
        below = rfirst[t][south_at]
        for c in range(chunks):
            lane = slice(c * LANES, (c + 1) * LANES)
            value = below[:, lane] + jnp.where(finer, beside[c:c + 1, :], 0.0)
            E[rows:rows + 1, lane] = jnp.where(south_ok, value, 0.0)
        share_n = rlast[t][north_at, 1 if t == 0 else 0]
        wet_n = rlast[0][north_at, 0]
        Q_to = Q1
        Q_to[7:8, :] = jnp.where(north_ok, share_n - COURANT * wet_n * E[0:1, :], 0.0)
        return jnp.transpose(tmp[...])

    make_messages(0)
    sides = (level > 0).astype(jnp.int32) + (level < levels - 1).astype(jnp.int32)
    pl.semaphore_wait(barrier, 2 * patches - 1 + 2 * patches * sides)
    send_messages(0)
    loads[7].wait()
    for r in range(0, rows - BLOCK, BLOCK):
        advance(r, E0, P0, Q0, H, W, None, E1, P1, Q1)
    halo = receive(0)
    for r in (0, rows - BLOCK):
        advance(r, E0, P0, Q0, H, W, None, E1, P1, Q1)
    head = slice(0, LANES)
    e = E0[0:rows, head]
    wet = W[:, head].astype(jnp.float32)
    p_edge = halo[:, 1:2] - COURANT * halo[:, 2:3] * e[:, 0:1]
    across = Q1[8:8 + rows, head] - Q1[7:7 + rows, head]
    fixed = wet * (e - COURANT * H[:, head] * ((P1[:, head] - p_edge) + across))
    E1[0:rows, head] = jnp.where(lane_ids == 0, fixed, E1[0:rows, head])
    e = E0[0:rows, tail]
    wet = W[:, tail].astype(jnp.float32)
    p = wet * (P0[:, tail] - COURANT * (halo[:, 0:1] - e))
    p = jnp.where(lane_ids == LANES - 1, p, P1[:, tail])
    P1[:, tail] = p
    across = Q1[8:8 + rows, tail] - Q1[7:7 + rows, tail]
    fixed = wet * (e - COURANT * H[:, tail] * ((p - pltpu.roll(p, 1, 1)) + across))
    E1[0:rows, tail] = jnp.where(lane_ids == LANES - 1, fixed, E1[0:rows, tail])

    make_messages(1)
    send_messages(1)
    for r in range(0, rows - BLOCK, BLOCK):
        advance(r, E1, P1, Q1, H, W, None, E2, P2, Q2)
    halo_out[...] = receive(1)
    for t in range(STEPS):
        each_halo(t, 1, 0, lambda copy: copy.wait_send(), True)

        @pl.when(level > 0)
        def _():
            inflow_send_waits(t)


def body(mesh, adjoint_height, adjoint_momenta, depth, wet_mask, adjacency, nest_gain, nest_index):
    patches, levels = mesh.shape["patch"], mesh.shape["level"]
    rows, cols = adjoint_height.shape[1:]
    chunks = cols // LANES
    f32 = jnp.float32
    anywhere = pl.BlockSpec(memory_space=pl.ANY)
    v = pltpu.VMEM
    dma = pltpu.SemaphoreType.DMA
    whole = (v((rows + 8, cols), f32), v((rows, cols), f32), v((rows + 8, cols), f32))
    scratch = [
        pltpu.SMEM(adjacency.shape, jnp.int32),
        *whole,
        v(nest_gain.shape, f32), v(nest_index.shape, jnp.int32),
        v((chunks, LANES), f32), v((chunks, LANES), jnp.int32), v((chunks, LANES), f32),
        v((8, LANES), f32),
        v((STEPS, 1, cols), f32), v((STEPS + 1, 1, cols), f32), v((STEPS, 8, LANES), f32),
        v((STEPS, chunks, LANES), f32), v((STEPS, 2, LANES), f32),
        v((STEPS, chunks, LANES), f32),
        dma((8,)), dma((STEPS, 5, patches)), dma((STEPS, 5, patches)), dma((STEPS, 2)),
    ]
    scratch += [v((patches, 1, cols), f32)] * STEPS
    scratch += [v((patches, 2 if t == 0 else 1, 1, cols), f32) for t in range(STEPS)]
    scratch += [v((patches, 8, LANES), f32)] * STEPS
    scratch += [v((patches, chunks, LANES), f32)] * STEPS
    scratch += [v((patches, 2, LANES), f32)] * STEPS
    here = pl.BlockSpec(memory_space=pltpu.VMEM)
    state = pl.pallas_call(
        functools.partial(exchange, patches, levels, rows, cols),
        out_shape=(*whole, v((rows, cols), f32), v((rows, cols), jnp.int32), v((rows, 8), f32), *whole),
        in_specs=[anywhere] * 7,
        out_specs=(here,) * 9,
        scratch_shapes=scratch,
        compiler_params=pltpu.CompilerParams(collective_id=0, has_side_effects=True,
                                             vmem_limit_bytes=12 << 20),
    )(*[pltpu.with_memory_space_constraint(x, pltpu.HBM) for x in (
        adjacency, adjoint_height, adjoint_momenta, depth, wet_mask, nest_gain, nest_index)])
    state = [pltpu.with_memory_space_constraint(x, pltpu.VMEM) for x in state]
    return pl.pallas_call(
        functools.partial(finish, rows),
        out_shape=(jax.ShapeDtypeStruct(adjoint_height.shape, f32),
                   jax.ShapeDtypeStruct(adjoint_momenta.shape, f32)),
        in_specs=[here] * 9,
        out_specs=(anywhere, anywhere),
        scratch_shapes=[*whole, dma((12,))],
        compiler_params=pltpu.CompilerParams(vmem_limit_bytes=12 << 20),
    )(*state)


def solution(mesh):
    in_specs = (
        P(("parts", "level"), ("patch", "sub"), None),
        P(None, ("parts", "level"), ("patch", "sub"), None),
        P("level", ("patch", "sub"), None),
        P("level", ("patch", "sub"), None),
        P("level", None, None),
        P(None, ("patch", "sub")),
        P(None, ("patch", "sub")),
    )
    out_specs = (
        P(("parts", "level"), ("patch", "sub"), None),
        P(None, ("parts", "level"), ("patch", "sub"), None),
    )
    return jax.shard_map(functools.partial(body, mesh), mesh=mesh, in_specs=in_specs,
                         out_specs=out_specs, check_vma=False)
```

```python
import functools

import jax
import jax.numpy as jnp
from jax import lax
from jax.experimental import pallas as pl
from jax.experimental.pallas import tpu as pltpu
from jax.sharding import PartitionSpec as P

STEPS = 2
COURANT = 0.45
LANES = 128
BLOCK = 8


def advance(r, E, Pm, Q, H, W, halo, E_to, P_to, Q_to):
    cols = Pm.shape[1]
    lane_ids = lax.broadcasted_iota(jnp.int32, (BLOCK, cols), 1)
    span = slice(r, r + BLOCK)
    e = E[span, :]
    wet = W[span, :].astype(jnp.float32)
    e_south = E[r + 1:r + 1 + BLOCK, :]
    e_east = pltpu.roll(e, cols - 1, 1)
    if halo is not None:
        e_east = jnp.where(lane_ids == cols - 1, halo[span, 0:1], e_east)
    p = wet * (Pm[span, :] - COURANT * (e_east - e))
    q = wet * (Q[8 + r:16 + r, :] - COURANT * (e_south - e))
    p_west = pltpu.roll(p, 1, 1)
    if halo is not None:
        p_edge = halo[span, 1:2] - COURANT * halo[span, 2:3] * e[:, 0:1]
        p_west = jnp.where(lane_ids == 0, p_edge, p_west)
    P_to[span, :] = p
    Q_to[8 + r:16 + r, :] = q
    q_north = Q_to[7 + r:15 + r, :]
    E_to[span, :] = wet * (e - COURANT * H[span, :] * ((p - p_west) + (q - q_north)))


def finish(rows, E, Pm, Q, H, W, halo, E2, P2, Q2, eta_out, mom_out, Ef, Pf, Qf, sems):
    cols = Pm.shape[1]
    end = rows - BLOCK
    mid = slice(BLOCK, end)
    head, tail = slice(0, LANES), slice(cols - LANES, cols)
    before, inner = slice(0, cols - LANES), slice(LANES, cols - LANES)
    stores = []

    def store(src, dst):
        copy = pltpu.make_async_copy(src, dst, sems.at[len(stores)])
        copy.start()
        stores.append(copy)

    eta_to, row_to, col_to = eta_out.at[0], mom_out.at[0, 0], mom_out.at[1, 0]
    store(Q2.at[BLOCK + 8:end + 8], col_to.at[mid])
    store(P2.at[mid, before], row_to.at[mid, before])
    store(E2.at[mid, inner], eta_to.at[mid, inner])
    edges = halo[...]
    lane_ids = lax.broadcasted_iota(jnp.int32, (end - BLOCK, LANES), 1)

    across = Q2[BLOCK + 8:end + 8, head] - Q2[BLOCK + 7:end + 7, head]
    e = E[mid, head]
    wet = W[mid, head].astype(jnp.float32)
    p_edge = edges[mid, 1:2] - COURANT * edges[mid, 2:3] * e[:, 0:1]
    fixed = wet * (e - COURANT * H[mid, head] * ((P2[mid, head] - p_edge) + across))
    Ef[mid, head] = jnp.where(lane_ids == 0, fixed, E2[mid, head])
    store(Ef.at[mid, head], eta_to.at[mid, head])

    across = Q2[BLOCK + 8:end + 8, tail] - Q2[BLOCK + 7:end + 7, tail]
    e = E[mid, tail]
    wet = W[mid, tail].astype(jnp.float32)
    p = wet * (Pm[mid, tail] - COURANT * (edges[mid, 0:1] - e))
    p = jnp.where(lane_ids == LANES - 1, p, P2[mid, tail])
    Pf[mid, tail] = p
    store(Pf.at[mid, tail], row_to.at[mid, tail])
    fixed = wet * (e - COURANT * H[mid, tail] * ((p - pltpu.roll(p, 1, 1)) + across))
    Ef[mid, tail] = jnp.where(lane_ids == LANES - 1, fixed, E2[mid, tail])
    store(Ef.at[mid, tail], eta_to.at[mid, tail])

    for r in (0, end):
        Qf[7 + r:8 + r, :] = (Q if r == 0 else Q2)[7 + r:8 + r, :]
        advance(r, E, Pm, Q, H, W, edges, Ef, Pf, Qf)
        at = slice(r, r + BLOCK)
        store(Pf.at[at], row_to.at[at])
        store(Qf.at[8 + r:16 + r], col_to.at[at])
        store(Ef.at[at], eta_to.at[at])
    for copy in stores:
        copy.wait()


def exchange(patches, levels, rows, cols,
             adj_hbm, eta_hbm, mom_hbm, depth_hbm, wet_hbm, gain_hbm, table_hbm,
             E1, P1, Q1, H, W, halo_out, E2, P2, Q2,
             adj, E0, P0, Q0, gain_v, table_v, f8, idx8, gain8, tmp,
             sfirst, slast, scol, sinf, sew,
             rown, in_sems, send_sems, recv_sems, own_sems, *landing):
    rfirst, rlast, rcol, rnbr, rew = (landing[n * STEPS:(n + 1) * STEPS] for n in range(5))
    fields = ((E0, P0, Q0), (E1, P1, Q1))
    patch = lax.axis_index("patch")
    level = lax.axis_index("level")
    half = lax.axis_index("sub")
    chunks = cols // LANES
    other = 1 - half

    loads = [
        pltpu.make_async_copy(eta_hbm.at[0], E0.at[0:rows], in_sems.at[0]),
        pltpu.make_async_copy(mom_hbm.at[0, 0], P0, in_sems.at[1]),
        pltpu.make_async_copy(mom_hbm.at[1, 0], Q0.at[8:8 + rows], in_sems.at[2]),
        pltpu.make_async_copy(wet_hbm.at[0], W, in_sems.at[3]),
        pltpu.make_async_copy(table_hbm, table_v, in_sems.at[4]),
        pltpu.make_async_copy(gain_hbm, gain_v, in_sems.at[5]),
        pltpu.make_async_copy(adj_hbm, adj, in_sems.at[6]),
        pltpu.make_async_copy(depth_hbm.at[0], H, in_sems.at[7]),
    ]
    barrier = pltpu.get_barrier_semaphore()

    peers = [patch] + [lax.rem(patch + d, patches) for d in range(1, patches)]

    def greet(d, h, lev):
        pl.semaphore_signal(barrier, inc=1, device_id={
            "patch": peers[d], "sub": h, "level": lev},
            device_id_type=pl.DeviceIdType.MESH)

    for d in range(patches - 1, -1, -1):
        greet(d, other, level)
        if d:
            greet(d, half, level)

    @pl.when(level > 0)
    def _():
        for d in range(patches):
            greet(d, half, level - 1)
            greet(d, other, level - 1)

    @pl.when(level < levels - 1)
    def _():
        for d in range(patches):
            greet(d, half, level + 1)
            greet(d, other, level + 1)

    for load in loads:
        load.start()

    for load in loads[:7]:
        load.wait()

    lower = jnp.maximum(level - 1, 0)
    for c in range(chunks):
        lane = slice(c * LANES, (c + 1) * LANES)
        index, gain = table_v[0:1, lane], gain_v[0:1, lane]
        for lev in range(1, levels - 1):
            index = jnp.where(lower == lev, table_v[lev:lev + 1, lane], index)
            gain = jnp.where(lower == lev, gain_v[lev:lev + 1, lane], gain)
        idx8[c:c + 1, :] = index
        gain8[c:c + 1, :] = gain

    def remote(t, kind, src, buf, slot, d, h, lev):
        return pltpu.make_async_remote_copy(
            src_ref=src, dst_ref=buf, send_sem=send_sems.at[t, kind, d],
            recv_sem=recv_sems.at[t, kind, slot],
            device_id={"patch": peers[d], "sub": h, "level": lev},
            device_id_type=pl.DeviceIdType.MESH)

    def last_part(t):
        return slice(0, 2) if t == 0 else slice(t + 1, t + 2)

    def column_copy(t, slot, d):
        return remote(t, 0, scol.at[t, 0:3], rcol[t].at[slot, 0:3], slot, d, half, level)

    def first_copy(t, slot, d):
        return remote(t, 1, sfirst.at[t], rfirst[t].at[slot], slot, d, other, level)

    def last_copy(t, slot, d):
        part = last_part(t)
        return remote(t, 2, slast.at[part], rlast[t].at[slot], slot, d, other, level)

    def beside_copy(t, slot, d):
        return remote(t, 3, sinf.at[t], rnbr[t].at[slot], slot, d, other, lower)

    def ends_copy(t, slot, d):
        return remote(t, 4, sew.at[t], rew[t].at[slot], slot, d, half, lower)

    def per_half(across, inside, act):
        @pl.when(half == across)
        def _():
            for d in range(1, patches):
                act(d)

        @pl.when(half == inside)
        def _():
            act(0)

    def own_copy(t):
        return pltpu.make_async_remote_copy(
            src_ref=sinf.at[t], dst_ref=rown.at[t], send_sem=own_sems.at[t, 0],
            recv_sem=own_sems.at[t, 1], device_id={"level": lower},
            device_id_type=pl.DeviceIdType.MESH)

    def make_inflow(t):
        E = fields[t][0]
        for c in range(chunks):
            f8[c:c + 1, :] = E[0:1, c * LANES:(c + 1) * LANES]
        index = idx8[...]
        inside = jnp.bitwise_and(index, LANES - 1)
        which = lax.shift_right_logical(index, 7)
        picked = jnp.zeros((chunks, LANES), jnp.float32)
        for c in range(chunks):
            source = jnp.broadcast_to(f8[c:c + 1, :], (chunks, LANES))
            got = jnp.take_along_axis(source, inside, axis=1, mode="promise_in_bounds")
            picked = jnp.where(which == c, got, picked)
        inflow = gain8[...] * picked
        sinf[t] = inflow
        sew[t, 0:1, :] = inflow[0:1, :]
        sew[t, 1:2, :] = pltpu.roll(inflow[chunks - 1:chunks, :], 1, 1)

    def send_inflow(t):
        own_copy(t).start()
        per_half(0, 1, lambda d: beside_copy(t, patch, d).start())
        for d in range(1, patches):
            ends_copy(t, patch, d).start()

    def inflow_waits(t):
        per_half(1, 0, lambda d: beside_copy(t, peers[d], d).wait_recv())
        for d in range(1, patches):
            ends_copy(t, peers[d], d).wait_recv()

    def inflow_send_waits(t):
        own_copy(t).wait_send()
        per_half(0, 1, lambda d: beside_copy(t, patch, d).wait_send())
        for d in range(1, patches):
            ends_copy(t, patch, d).wait_send()

    def send_halos(t, act):
        send_rows(t, act)
        send_columns(t, act)

    def send_columns(t, act):
        for d in range(1, patches):
            act(column_copy(t, patch, d))

    def send_rows(t, act):
        @pl.when(half == 0)
        def _():
            for d in range(1, patches):
                act(first_copy(t, patch, d))
            act(last_copy(t, patch, 0))

        @pl.when(half == 1)
        def _():
            for d in range(1, patches):
                act(last_copy(t, patch, d))
            act(first_copy(t, patch, 0))

    def receive_halos(t):
        @pl.when(half == 0)
        def _():
            first_copy(t, peers[0], 0).wait_recv()
            for d in range(1, patches):
                last_copy(t, peers[d], d).wait_recv()

        @pl.when(half == 1)
        def _():
            last_copy(t, peers[0], 0).wait_recv()
            for d in range(1, patches):
                first_copy(t, peers[d], d).wait_recv()

        for d in range(1, patches):
            column_copy(t, peers[d], d).wait_recv()

    north = adj[0, patch, 0]
    south = adj[0, patch, 1]
    west = adj[0, patch, 2]
    east = adj[0, patch, 3]
    south_ok = jnp.logical_or(half == 0, south >= 0)
    north_ok = jnp.logical_or(half == 1, north >= 0)
    south_at = jnp.where(half == 0, patch, jnp.maximum(south, 0))
    north_at = jnp.where(half == 1, patch, jnp.maximum(north, 0))
    west_at = jnp.maximum(west, 0)
    east_at = jnp.maximum(east, 0)
    finer = level < levels - 1
    lane_ids = lax.broadcasted_iota(jnp.int32, (rows, LANES), 1)
    first_lane = lax.broadcasted_iota(jnp.int32, (1, LANES), 1) == 0
    tail = slice(cols - LANES, cols)
    end = rows - 1

    def make_messages(t):
        @pl.when(level == levels - 1)
        def _():
            make_inflow(t)

        make_rows(t)
        make_columns(t)

    def make_rows(t):
        E, Pm, Q = fields[t]
        sfirst[t] = E[0:1, :]
        wet_row = W[end:rows, :].astype(jnp.float32)
        slast[t + 1] = wet_row * (Q[8 + end:8 + rows, :] + COURANT * E[end:rows, :])
        if t == 0:
            slast[0] = wet_row

    def make_columns(t):
        E, Pm, Q = fields[t]
        wet_tail = W[:, tail].astype(jnp.float32)
        share = wet_tail * (Pm[:, tail] + COURANT * E[0:rows, tail])
        mixed = jnp.where(lane_ids == 0, E[0:rows, 0:LANES],
                          jnp.where(lane_ids == 1, pltpu.roll(share, 2, 1),
                                    pltpu.roll(wet_tail, 3, 1)))
        scol[t] = jnp.transpose(mixed[:, 0:8])

    def send_messages(t):
        @pl.when(level == levels - 1)
        def _():
            send_inflow(t)

        send_halos(t, lambda copy: copy.start())

    def receive(t):
        E, Pm, Q = fields[t]

        @pl.when(finer)
        def _():
            own_copy(t).wait_recv()
            for c in range(chunks):
                lane = slice(c * LANES, (c + 1) * LANES)
                E[0:1, lane] += rown[t, c:c + 1, :]

        if levels > 2:
            @pl.when(jnp.logical_and(level > 0, level < levels - 1))
            def _():
                make_inflow(t)
                send_inflow(t)

        receive_halos(t)

        @pl.when(finer)
        def _():
            inflow_waits(t)

        east_row = rcol[t][east_at][0:1, :]
        east_row += jnp.where(jnp.logical_and(first_lane, finer), rew[t][east_at][0:1, :], 0.0)
        west_cols = rcol[t][west_at]
        share = west_cols[1:2, :]
        wet_w = west_cols[2:3, :]
        share += jnp.where(jnp.logical_and(first_lane, finer),
                           COURANT * wet_w * rew[t][west_at][1:2, :], 0.0)
        tmp[0:1, :] = jnp.where(east >= 0, east_row, 0.0)
        tmp[1:2, :] = jnp.where(west >= 0, share, 0.0)
        tmp[2:3, :] = jnp.where(west >= 0, wet_w, 0.0)
        beside = rnbr[t][south_at]
        below = rfirst[t][south_at]
        for c in range(chunks):
            lane = slice(c * LANES, (c + 1) * LANES)
            value = below[:, lane] + jnp.where(finer, beside[c:c + 1, :], 0.0)
            E[rows:rows + 1, lane] = jnp.where(south_ok, value, 0.0)
        share_n = rlast[t][north_at, 1 if t == 0 else 0]
        wet_n = rlast[0][north_at, 0]
        Q_to = Q1
        Q_to[7:8, :] = jnp.where(north_ok, share_n - COURANT * wet_n * E[0:1, :], 0.0)
        return jnp.transpose(tmp[...])

    make_messages(0)
    sides = (level > 0).astype(jnp.int32) + (level < levels - 1).astype(jnp.int32)
    pl.semaphore_wait(barrier, 2 * patches - 1 + 2 * patches * sides)
    send_messages(0)
    loads[7].wait()
    for r in range(0, rows - BLOCK, BLOCK):
        advance(r, E0, P0, Q0, H, W, None, E1, P1, Q1)
    halo = receive(0)
    for r in (0, rows - BLOCK):
        advance(r, E0, P0, Q0, H, W, None, E1, P1, Q1)
    head = slice(0, LANES)
    e = E0[0:rows, head]
    wet = W[:, head].astype(jnp.float32)
    p_edge = halo[:, 1:2] - COURANT * halo[:, 2:3] * e[:, 0:1]
    across = Q1[8:8 + rows, head] - Q1[7:7 + rows, head]
    fixed = wet * (e - COURANT * H[:, head] * ((P1[:, head] - p_edge) + across))
    E1[0:rows, head] = jnp.where(lane_ids == 0, fixed, E1[0:rows, head])
    e = E0[0:rows, tail]
    wet = W[:, tail].astype(jnp.float32)
    p = wet * (P0[:, tail] - COURANT * (halo[:, 0:1] - e))
    p = jnp.where(lane_ids == LANES - 1, p, P1[:, tail])
    P1[:, tail] = p
    across = Q1[8:8 + rows, tail] - Q1[7:7 + rows, tail]
    fixed = wet * (e - COURANT * H[:, tail] * ((p - pltpu.roll(p, 1, 1)) + across))
    E1[0:rows, tail] = jnp.where(lane_ids == LANES - 1, fixed, E1[0:rows, tail])

    @pl.when(level == levels - 1)
    def _():
        make_inflow(1)
        send_inflow(1)

    make_rows(1)
    send_rows(1, lambda copy: copy.start())
    make_columns(1)
    send_columns(1, lambda copy: copy.start())
    for r in range(0, rows - BLOCK, BLOCK):
        advance(r, E1, P1, Q1, H, W, None, E2, P2, Q2)
    halo_out[...] = receive(1)
    for t in range(STEPS):
        send_halos(t, lambda copy: copy.wait_send())

        @pl.when(level > 0)
        def _():
            inflow_send_waits(t)


def body(mesh, adjoint_height, adjoint_momenta, depth, wet_mask, adjacency, nest_gain, nest_index):
    patches, levels = mesh.shape["patch"], mesh.shape["level"]
    rows, cols = adjoint_height.shape[1:]
    chunks = cols // LANES
    f32 = jnp.float32
    anywhere = pl.BlockSpec(memory_space=pl.ANY)
    v = pltpu.VMEM
    dma = pltpu.SemaphoreType.DMA
    whole = (v((rows + 8, cols), f32), v((rows, cols), f32), v((rows + 8, cols), f32))
    scratch = [
        pltpu.SMEM(adjacency.shape, jnp.int32),
        *whole,
        v(nest_gain.shape, f32), v(nest_index.shape, jnp.int32),
        v((chunks, LANES), f32), v((chunks, LANES), jnp.int32), v((chunks, LANES), f32),
        v((8, LANES), f32),
        v((STEPS, 1, cols), f32), v((STEPS + 1, 1, cols), f32), v((STEPS, 8, LANES), f32),
        v((STEPS, chunks, LANES), f32), v((STEPS, 2, LANES), f32),
        v((STEPS, chunks, LANES), f32),
        dma((8,)), dma((STEPS, 5, patches)), dma((STEPS, 5, patches)), dma((STEPS, 2)),
    ]
    scratch += [v((patches, 1, cols), f32)] * STEPS
    scratch += [v((patches, 2 if t == 0 else 1, 1, cols), f32) for t in range(STEPS)]
    scratch += [v((patches, 8, LANES), f32)] * STEPS
    scratch += [v((patches, chunks, LANES), f32)] * STEPS
    scratch += [v((patches, 2, LANES), f32)] * STEPS
    here = pl.BlockSpec(memory_space=pltpu.VMEM)
    state = pl.pallas_call(
        functools.partial(exchange, patches, levels, rows, cols),
        out_shape=(*whole, v((rows, cols), f32), v((rows, cols), jnp.int32), v((rows, 8), f32), *whole),
        in_specs=[anywhere] * 7,
        out_specs=(here,) * 9,
        scratch_shapes=scratch,
        compiler_params=pltpu.CompilerParams(collective_id=0, has_side_effects=True,
                                             vmem_limit_bytes=12 << 20),
    )(*[pltpu.with_memory_space_constraint(x, pltpu.HBM) for x in (
        adjacency, adjoint_height, adjoint_momenta, depth, wet_mask, nest_gain, nest_index)])
    state = [pltpu.with_memory_space_constraint(x, pltpu.VMEM) for x in state]
    return pl.pallas_call(
        functools.partial(finish, rows),
        out_shape=(jax.ShapeDtypeStruct(adjoint_height.shape, f32),
                   jax.ShapeDtypeStruct(adjoint_momenta.shape, f32)),
        in_specs=[here] * 9,
        out_specs=(anywhere, anywhere),
        scratch_shapes=[*whole, dma((12,))],
        compiler_params=pltpu.CompilerParams(vmem_limit_bytes=12 << 20),
    )(*state)


def solution(mesh):
    in_specs = (
        P(("parts", "level"), ("patch", "sub"), None),
        P(None, ("parts", "level"), ("patch", "sub"), None),
        P("level", ("patch", "sub"), None),
        P("level", ("patch", "sub"), None),
        P("level", None, None),
        P(None, ("patch", "sub")),
        P(None, ("patch", "sub")),
    )
    out_specs = (
        P(("parts", "level"), ("patch", "sub"), None),
        P(None, ("parts", "level"), ("patch", "sub"), None),
    )
    return jax.shard_map(functools.partial(body, mesh), mesh=mesh, in_specs=in_specs,
                         out_specs=out_specs, check_vma=False)
```
